512 devices in a mesh: prow: 16 (over z_lo, x, core), pcol: 32 (over y, z_hi).
Axes of the slice: x: 4, y: 8, z: 8 (z_hi: 4, z_lo: 2; z = z_hi * 2 + z_lo), core: 2. Of those that a mesh axis runs over, the one named last changes fastest.
Arguments:
- matrix: float32 [6, 16, 128, 3, 32, 128], P(None, 'prow', None, None, 'pcol'), may hold values from -1 to 40, as said below
- row_codes: int32 [6, 16, 128], P(None, 'prow'), may hold values from 1 to 8
- col_codes: int32 [3, 32, 128], P(None, 'pcol'), may hold values from 1 to 8
- fault_tiles: int32 [96, 2], replicated, may hold values from 0 to 95, as said below
- fault_cells: int32 [96, 2], replicated, may hold values from 0 to 127
- fault_bits: int32 [96], replicated, may hold values from 1 to 2
Outputs:
- factored: float32 [6, 16, 128, 3, 32, 128], P(None, 'prow', None, None, 'pcol')
- col_check: float32 [3, 32, 128], P(None, 'pcol')
- row_check: float32 [6, 16, 128], P(None, 'prow')
- col_flags: float32 [3, 32], P(None, 'pcol')
- row_flags: float32 [6, 16], P(None, 'prow')
The draws below stay inside these ranges and needn't reach their ends.
Inputs may be any that keep to these rules, and one draw needn't show every extreme that they name: `matrix`: symmetric positive definite. `fault_tiles`: each tile row index appears in exactly one fault, and so does each tile column index.
All inputs are finite; a program needn't handle non-finite values.
Results may differ from the reference program's by a relative error of at most 0.0003.
Values sent between devices are 32-bit elements; how exact they have to be, the bound alone decides.
No kernel may reach another device: no remote copies, remote signals or barrier semaphores. Data moves between devices by JAX's collectives and lax.ppermute only.
A program may use at most 64 MiB of HBM per device.

```python
import math
import jax
import jax.numpy as jnp
from jax import lax

TILE = 128
ORDER = 12288
TILES = 96
STEPS = 2
FAULTS = 96
N_PROW = 16
N_PCOL = 32


def draw_matrix(key, part):
    spread_bound = 2.6 / math.sqrt(ORDER)
    perturb = jax.random.uniform(jax.random.fold_in(key, 11), (ORDER, ORDER), jnp.float32, -spread_bound, spread_bound)
    symmetric = (perturb + perturb.T) * 0.5
    diagonal_lift = jax.random.uniform(jax.random.fold_in(key, 12), (ORDER,), jnp.float32, 4.0, 8.0)
    diagonal_index = jnp.arange(ORDER, dtype=jnp.int32)
    symmetric = symmetric.at[diagonal_index, diagonal_index].add(diagonal_lift)
    return symmetric.reshape(TILES // N_PROW, N_PROW, TILE, TILES // N_PCOL, N_PCOL, TILE)


def draw_fault_tiles(key, part):
    fault_rows = jax.random.permutation(jax.random.fold_in(key, 21), TILES)
    fault_cols = jax.random.permutation(jax.random.fold_in(key, 22), TILES)
    return jnp.stack([fault_rows, fault_cols], axis=1).astype(jnp.int32)


def set_ends(result, key, least, top_value):
    longest = result.shape.index(max(result.shape))
    spots = []
    for shift in (0, 1):
        where = [jax.random.randint(jax.random.fold_in(key, axis), (), 0, length) for axis, length in enumerate(result.shape)]
        where[longest] = (where[longest] + shift) % result.shape[longest]
        spots.append(tuple(where))
    return result.at[spots[0]].set(least).at[spots[1]].set(top_value)


def setup_inputs(seed: int = 0) -> dict:
    splits = jax.random.split(jax.random.key(seed), 7)
    return {
        "matrix": draw_matrix(jax.random.fold_in(splits[6], 71), 0),
        "row_codes": set_ends(jax.random.randint(splits[1], (TILES // N_PROW, N_PROW, TILE), 1, 9), jax.random.fold_in(splits[1], 1), 1, 8).astype(jnp.int32),
        "col_codes": set_ends(jax.random.randint(splits[2], (TILES // N_PCOL, N_PCOL, TILE), 1, 9), jax.random.fold_in(splits[2], 1), 1, 8).astype(jnp.int32),
        "fault_tiles": draw_fault_tiles(jax.random.fold_in(splits[6], 71), 0),
        "fault_cells": set_ends(jax.random.randint(splits[4], (FAULTS, 2), 0, TILE), jax.random.fold_in(splits[4], 1), 0, TILE - 1).astype(jnp.int32),
        "fault_bits": set_ends(jax.random.randint(splits[5], (FAULTS,), 1, 3), jax.random.fold_in(splits[5], 1), 1, 2).astype(jnp.int32),
    }


precise = lax.Precision.HIGHEST

def reference(matrix, row_codes, col_codes, fault_tiles, fault_cells, fault_bits):
    whole_matrix = matrix.reshape(ORDER, ORDER)
    row_weights = row_codes.reshape(ORDER).astype(jnp.float32) * 0.25
    col_weights = col_codes.reshape(ORDER).astype(jnp.float32) * 0.25
    col_check = jnp.dot(row_weights, whole_matrix, precision=precise)
    row_check = jnp.dot(whole_matrix, col_weights, precision=precise)
    magnitude = jnp.exp2(fault_bits.astype(jnp.float32) - 1.0)
    fault_rows = (fault_tiles[:, 0] * TILE + fault_cells[:, 0]).astype(jnp.int32)
    fault_cols = (fault_tiles[:, 1] * TILE + fault_cells[:, 1]).astype(jnp.int32)
    whole_matrix = whole_matrix.at[fault_rows, fault_cols].add(magnitude)
    tile_index = jnp.arange(ORDER, dtype=jnp.int32) // TILE
    identity = jnp.eye(TILE, dtype=jnp.float32)
    for step_index in range(STEPS):
        first_row = step_index * TILE
        diagonal = whole_matrix[first_row:first_row + TILE, first_row:first_row + TILE]
        factor = jnp.linalg.cholesky(diagonal)
        inverse = jax.scipy.linalg.solve_triangular(factor, identity, lower=True)
        product = jnp.dot(whole_matrix[:, first_row:first_row + TILE], inverse.T, precision=precise)
        panel_cols = jnp.where((tile_index > step_index)[:, None], product, 0.0)
        panel_cols = panel_cols.at[first_row:first_row + TILE].set(factor)
        new_check = jnp.dot(inverse, col_check[first_row:first_row + TILE], precision=precise)
        shift_vector = jnp.dot(col_weights, panel_cols, precision=precise) - col_weights[first_row:first_row + TILE]
        row_check = row_check - jnp.dot(panel_cols, shift_vector, precision=precise)
        col_check = col_check - jnp.where(tile_index > step_index, jnp.dot(panel_cols, new_check, precision=precise), 0.0)
        col_check = col_check.at[first_row:first_row + TILE].set(new_check)
        trailing_panel = jnp.where((tile_index > step_index)[:, None], panel_cols, 0.0)
        whole_matrix = whole_matrix - jnp.dot(trailing_panel, trailing_panel.T, precision=precise)
        whole_matrix = whole_matrix.at[:, first_row:first_row + TILE].set(panel_cols)
        cleared = (tile_index == step_index)[:, None] & (tile_index > step_index)[None, :]
        whole_matrix = jnp.where(cleared, 0.0, whole_matrix)
    col_found = jnp.dot(row_weights, whole_matrix, precision=precise)
    row_found = jnp.dot(whole_matrix, col_weights, precision=precise)
    col_flags = jnp.max(jnp.abs(col_check - col_found).reshape(TILES, TILE), axis=1)
    row_flags = jnp.max(jnp.abs(row_check - row_found).reshape(TILES, TILE), axis=1)
    return (whole_matrix.reshape(matrix.shape), col_check.reshape(TILES // N_PCOL, N_PCOL, TILE), row_check.reshape(TILES // N_PROW, N_PROW, TILE), col_flags.reshape(TILES // N_PCOL, N_PCOL), row_flags.reshape(TILES // N_PROW, N_PROW))
```

```python
import jax
import jax.numpy as jnp
from jax import lax
from jax.sharding import PartitionSpec as P

precise = lax.Precision.HIGHEST


def dot(spec, a, b):
    return jnp.einsum(spec, a, b, precision=precise)


def factor_tile(tile):
    factor = jnp.linalg.cholesky(tile)
    identity = jnp.eye(tile.shape[0], dtype=jnp.float32)
    inverse = jax.scipy.linalg.solve_triangular(factor, identity, lower=True)
    return factor, inverse


def exchange(message, axis):
    return lax.all_to_all(message, axis, 0, 0, tiled=True)


def everyone(part, count):
    return jnp.broadcast_to(part[None], (count,) + part.shape)


def local(matrix, row_codes, col_codes, fault_tiles, fault_cells, fault_bits):
    grid_rows = lax.axis_size("prow")
    grid_cols = lax.axis_size("pcol")
    grid_row = lax.axis_index("prow")
    grid_col = lax.axis_index("pcol")
    rows, _, size, cols, _, _ = matrix.shape
    share = size // grid_rows
    fold = grid_cols // grid_rows
    blocks = matrix.reshape(rows, size, cols, size)
    row_weights = row_codes.reshape(rows, size).astype(jnp.float32) * 0.25
    col_weights = col_codes.reshape(cols, size).astype(jnp.float32) * 0.25
    tile_row = jnp.arange(rows, dtype=jnp.int32) * grid_rows + grid_row
    tile_col = jnp.arange(cols, dtype=jnp.int32) * grid_cols + grid_col

    magnitude = jnp.exp2(fault_bits.astype(jnp.float32) - 1.0)
    fault_rows = fault_tiles[:, 0] * size + fault_cells[:, 0]
    fault_cols = fault_tiles[:, 1] * size + fault_cells[:, 1]
    offsets = jnp.arange(size, dtype=jnp.int32)
    local_rows = (tile_row[:, None] * size + offsets[None, :]).reshape(-1)
    local_cols = (tile_col[:, None] * size + offsets[None, :]).reshape(-1)
    hit_rows = (fault_rows[:, None] == local_rows[None, :]).astype(jnp.float32) * magnitude[:, None]
    hit_cols = (fault_cols[:, None] == local_cols[None, :]).astype(jnp.float32)
    faults_added = dot("fr,fc->rc", hit_rows, hit_cols).reshape(rows, size, cols, size)
    mirror_rows = (fault_cols[:, None] == local_rows[None, :size]).astype(jnp.float32)
    mirror_cols = (fault_rows[:, None] == local_cols[None, :]).astype(jnp.float32) * magnitude[:, None]
    mirrored = dot("fr,fc->rc", mirror_rows, mirror_cols).reshape(size, cols, size)

    col_part = dot("ia,iajc->jc", row_weights, blocks)
    row_part = dot("iajc,jc->ia", blocks, col_weights)
    strip = blocks[0] + mirrored
    below = jnp.where((tile_col > grid_row)[:, None], col_weights, 0.0)
    panel_part = dot("ajc,jc->a", strip, below)[None]

    pieces = strip.reshape(grid_rows, share, cols, size).transpose(0, 2, 1, 3)
    message = jnp.concatenate(
        [
            pieces.reshape(grid_rows, cols * share, size),
            everyone(jnp.concatenate([col_part, panel_part]), grid_rows),
        ],
        axis=1,
    )
    first = exchange(message, "prow")
    own_share = first[:2, : cols * share].reshape(2 * cols * share, size)
    col_check = jnp.sum(first[:, cols * share : cols * share + cols], axis=0)
    panel_part = first[:2, cols * share + cols]

    message = jnp.concatenate([own_share, row_part, panel_part, col_check[:1], col_weights[:1]])
    second = exchange(everyone(message, grid_cols), "pcol")
    depth = 2 * cols * share
    shares = second[:, :depth]
    row_check = jnp.sum(second[:, depth : depth + rows], axis=0)
    panel_sum = jnp.sum(second[:, depth + rows : depth + rows + 2], axis=0)
    check_0, check_1 = second[0, depth + rows + 2], second[1, depth + rows + 2]
    weight_0, weight_1 = second[0, depth + rows + 3], second[1, depth + rows + 3]

    by_row = shares.reshape(fold, grid_rows, depth, size).transpose(1, 0, 2, 3)
    corner = jnp.concatenate(
        [shares[0, :share], shares[1, :share], shares[1, cols * share : cols * share + share]]
    )
    message = jnp.concatenate(
        [
            by_row.reshape(grid_rows, fold * depth, size),
            everyone(jnp.concatenate([own_share, corner]), grid_rows),
        ],
        axis=1,
    )
    third = exchange(message, "prow")
    row_panel = third[:, : fold * depth].reshape(grid_rows, fold, 2, cols, share, size)
    row_panel = row_panel.transpose(2, 0, 4, 3, 1, 5).reshape(2, size, rows, size)
    col_panel = third[:, fold * depth : (fold + 1) * depth].reshape(grid_rows, 2, cols, share, size)
    col_panel = col_panel.transpose(1, 0, 3, 2, 4).reshape(2, size, cols, size)
    corner = third[:, (fold + 1) * depth :].reshape(grid_rows, 3, share, size)
    corner = corner.transpose(1, 0, 2, 3).reshape(3, size, size)

    factor_0, inverse_0 = factor_tile(corner[0])
    below_0 = dot("ab,bc->ac", inverse_0, corner[1])
    factor_1, inverse_1 = factor_tile(corner[2] - dot("ba,bc->ac", below_0, below_0))
    mixed = -dot("ab,bc->ac", inverse_1, dot("ba,bc->ac", below_0, inverse_0))
    transform = jnp.concatenate(
        [
            jnp.concatenate([inverse_0, jnp.zeros_like(inverse_0)], axis=1),
            jnp.concatenate([mixed, inverse_1], axis=1),
        ]
    )
    factors = jnp.stack([factor_0.T, factor_1.T])

    steps = jnp.arange(2, dtype=jnp.int32)

    def panels(raw, tiles):
        product = dot("ab,bc->ac", transform, raw.reshape(2 * size, -1))
        product = product.reshape(2, size, tiles.shape[0], size)
        after = (tiles[None, :] > steps[:, None])[:, None, :, None]
        level = (tiles[None, :] == steps[:, None])[:, None, :, None]
        trailing = jnp.where(after, product, 0.0)
        return trailing, jnp.where(level, factors[:, :, None, :], trailing)

    row_trailing, row_full = panels(row_panel, tile_row)
    col_trailing, _ = panels(col_panel, tile_col)

    new_0 = dot("ab,b->a", inverse_0, check_0)
    new_1 = dot("ab,b->a", inverse_1, check_1 - dot("ba,b->a", below_0, new_0))
    shift_0 = dot("ab,b->a", inverse_0, panel_sum[0]) + dot("ba,b->a", factor_0, weight_0) - weight_0
    rest = dot("ab,b->a", inverse_0, panel_sum[0] - dot("ab,b->a", corner[1], weight_1))
    shift_1 = dot("ab,b->a", inverse_1, panel_sum[1] - dot("ba,b->a", below_0, rest))
    shift_1 = shift_1 + dot("ba,b->a", factor_1, weight_1) - weight_1
    new = jnp.stack([new_0, new_1])
    shift = jnp.stack([shift_0, shift_1])
    row_check = row_check - dot("kbia,kb->ia", row_full, shift)
    col_check = col_check - dot("kbja,kb->ja", col_trailing, new)
    col_check = jnp.where((tile_col == 0)[:, None], new_0, col_check)
    col_check = jnp.where((tile_col == 1)[:, None], new_1, col_check)

    update = dot(
        "br,bc->rc",
        row_trailing.reshape(2 * size, rows * size),
        col_trailing.reshape(2 * size, cols * size),
    )
    blocks = blocks + faults_added - update.reshape(rows, size, cols, size)
    settled = jnp.where(grid_col == 0, row_full[0], row_full[1]).transpose(1, 2, 0)
    blocks = jnp.concatenate(
        [jnp.where(grid_col < 2, settled, blocks[:, :, 0])[:, :, None], blocks[:, :, 1:]], axis=2
    )
    cleared = (tile_row < 2)[:, None] & (tile_col[None, :] > tile_row[:, None])
    blocks = jnp.where(cleared[:, None, :, None], 0.0, blocks)

    col_part = dot("ia,iajc->jc", row_weights, blocks)
    row_part = dot("iajc,jc->ia", blocks, col_weights)
    col_found = jnp.sum(exchange(everyone(col_part, grid_rows), "prow"), axis=0)
    row_found = jnp.sum(exchange(everyone(row_part, grid_cols), "pcol"), axis=0)
    col_flags = jnp.max(jnp.abs(col_check - col_found), axis=1)
    row_flags = jnp.max(jnp.abs(row_check - row_found), axis=1)
    return (
        blocks.reshape(matrix.shape),
        col_check.reshape(cols, 1, size),
        row_check.reshape(rows, 1, size),
        col_flags.reshape(cols, 1),
        row_flags.reshape(rows, 1),
    )


def solution(mesh):
    return jax.shard_map(
        local,
        mesh=mesh,
        in_specs=(
            P(None, "prow", None, None, "pcol", None),
            P(None, "prow", None),
            P(None, "pcol", None),
            P(),
            P(),
            P(),
        ),
        out_specs=(
            P(None, "prow", None, None, "pcol", None),
            P(None, "pcol", None),
            P(None, "prow", None),
            P(None, "pcol"),
            P(None, "prow"),
        ),
        check_vma=False,
    )
```

```python
import functools

import jax
import jax.numpy as jnp
from jax import lax
from jax.experimental import pallas as pl
from jax.experimental.pallas import tpu as pltpu
from jax.sharding import PartitionSpec as P

SIZE = 128
GROUP = 8
precise = lax.Precision.HIGHEST
VMEM = pl.BlockSpec(memory_space=pltpu.VMEM)
SMEM = pl.BlockSpec(memory_space=pltpu.SMEM)


def exchange(message, axis):
    return lax.all_to_all(message, axis, 0, 0, tiled=True)


def everyone(part, count):
    return jnp.broadcast_to(part[None], (count,) + part.shape)


def mm(a, b):
    return jnp.dot(a, b, precision=precise, preferred_element_type=jnp.float32)


def mm_nt(a, b):
    return lax.dot_general(
        a, b, (((1,), (1,)), ((), ())), precision=precise, preferred_element_type=jnp.float32
    )


def factor_tile(tile):
    lanes = lambda v, c: jnp.broadcast_to(v[:, c : c + 1], v.shape)
    rows = lambda v, j: jnp.broadcast_to(v[j : j + 1, :], v.shape)
    groups = SIZE // GROUP
    sub = lax.broadcasted_iota(jnp.int32, (GROUP, SIZE), 0)
    lan = lax.broadcasted_iota(jnp.int32, (GROUP, SIZE), 1)
    left = [tile[GROUP * i : GROUP * (i + 1), :] for i in range(groups)]
    right = [jnp.where(lan == sub + GROUP * i, 1.0, 0.0) for i in range(groups)]
    upper, inverse = [], []
    for b in range(groups):
        first = GROUP * b
        column = [lanes(left[b], first + j) for j in range(GROUP)]
        d = [[rows(column[j], i) if j <= i else None for j in range(GROUP)] for i in range(GROUP)]
        ra = [rows(left[b], j) for j in range(GROUP)]
        rb = [rows(right[b], j) for j in range(GROUP)]
        scale = []
        for k in range(GROUP):
            scale.append(lax.rsqrt(d[k][k]))
            for i in range(k + 1, GROUP):
                d[i][k] = d[i][k] * scale[k]
            for j in range(k + 1, GROUP):
                for i in range(j, GROUP):
                    d[i][j] = d[i][j] - d[i][k] * d[j][k]
        for j in range(GROUP):
            for k in range(j):
                ra[j] = ra[j] - d[j][k] * ra[k]
                rb[j] = rb[j] - d[j][k] * rb[k]
            ra[j] = ra[j] * scale[j]
            rb[j] = rb[j] * scale[j]
        for i in range(b + 1, groups):
            c = [lanes(left[i], first + j) for j in range(GROUP)]
            for j in range(GROUP):
                for k in range(j):
                    c[j] = c[j] - d[j][k] * c[k]
                c[j] = c[j] * scale[j]
            for j in range(GROUP):
                left[i] = left[i] - c[j] * ra[j]
                right[i] = right[i] - c[j] * rb[j]
        out_a, out_b = ra[GROUP - 1], rb[GROUP - 1]
        for j in range(GROUP - 1):
            out_a = jnp.where(sub == j, ra[j], out_a)
            out_b = jnp.where(sub == j, rb[j], out_b)
        upper.append(jnp.where(lan >= sub + first, out_a, 0.0))
        inverse.append(out_b)
    return jnp.concatenate(upper), jnp.concatenate(inverse)


def columns_of(weights):
    count = weights.shape[0]
    padded = jnp.concatenate([weights, jnp.zeros((SIZE - count, SIZE), jnp.float32)])
    turned = padded.T
    return [jnp.broadcast_to(turned[:, t : t + 1], (SIZE, SIZE)) for t in range(count)]


def hits(fault_row, first, scale=None):
    place = first + lax.broadcasted_iota(jnp.int32, (SIZE, SIZE), 0)
    found = jnp.where(fault_row == place, 1.0 if scale is None else scale, 0.0)
    return found.astype(jnp.bfloat16)


def fault_tile(row_hits, col_hits):
    return lax.dot_general(
        row_hits, col_hits, (((1,), (1,)), ((), ())), preferred_element_type=jnp.float32
    )


def pre_kernel(geometry, place, faults, matrix, row_codes, col_codes, message, row_part):
    rows, cols, grid_rows, grid_cols = geometry
    grid_row, grid_col = place[0], place[1]
    share = SIZE // grid_rows
    row_weights = row_codes[...].astype(jnp.float32) * 0.25
    col_weights = col_codes[...].astype(jnp.float32) * 0.25
    turned = columns_of(row_weights)
    ones = jnp.ones((8, SIZE), jnp.float32)
    fault_row, fault_col = faults[0:1, :], faults[1:2, :]
    magnitude = faults[2:3, :].astype(jnp.float32)
    mirror_rows = hits(fault_col, grid_row * SIZE)
    col_sums = [jnp.zeros((SIZE, SIZE), jnp.float32) for _ in range(cols)]
    panel = jnp.zeros((SIZE, SIZE), jnp.float32)
    for t in range(rows):
        total = jnp.zeros((SIZE, SIZE), jnp.float32)
        for u in range(cols):
            tile = matrix[pl.ds(t * SIZE * cols + u, SIZE, cols), :]
            weight = col_weights[u : u + 1]
            total = total + tile * weight
            col_sums[u] = col_sums[u] + tile * turned[t]
            if t == 0:
                col_tile = u * grid_cols + grid_col
                tile = tile + fault_tile(mirror_rows, hits(fault_row, col_tile * SIZE, magnitude))
                panel = panel + tile * jnp.where(col_tile > grid_row, weight, 0.0)
                for i in range(grid_rows):
                    message[i, u * share : (u + 1) * share, :] = tile[i * share : (i + 1) * share]
        row_part[t : t + 1, :] = mm_nt(ones, total)[0:1]
    row_part[rows:8, :] = jnp.zeros((8 - rows, SIZE), jnp.float32)
    sums = [jnp.sum(col_sums[u], axis=0, keepdims=True) for u in range(cols)]
    sums.append(mm_nt(ones, panel)[0:1])
    sums.append(jnp.zeros((8 - cols - 1, SIZE), jnp.float32))
    sums = jnp.concatenate(sums)
    for i in range(grid_rows):
        message[i, cols * share : cols * share + 8, :] = sums


def post_kernel(
    geometry,
    place,
    faults,
    third,
    vectors,
    row_sums,
    col_sums,
    matrix,
    row_codes,
    col_codes,
    factored,
    col_check,
    row_check,
    col_message,
    row_message,
):
    rows, cols, grid_rows, grid_cols = geometry
    grid_row, grid_col = place[0], place[1]
    share = SIZE // grid_rows
    fold = grid_cols // grid_rows
    depth = 2 * cols * share

    def gathered(start):
        return jnp.concatenate([third[i, start : start + share, :] for i in range(grid_rows)])

    corner = [gathered((fold + 1) * depth + k * share) for k in range(3)]
    tile_0 = (corner[0] + corner[0].T) * 0.5
    upper_0, inverse_0 = factor_tile(tile_0)
    below_0 = mm(inverse_0, corner[1])
    tile_1 = corner[2] - mm(below_0.T, below_0)
    upper_1, inverse_1 = factor_tile((tile_1 + tile_1.T) * 0.5)
    mixed = -mm(inverse_1, mm(below_0.T, inverse_0))
    transform = jnp.concatenate(
        [
            jnp.concatenate([inverse_0, jnp.zeros_like(inverse_0)], axis=1),
            jnp.concatenate([mixed, inverse_1], axis=1),
        ]
    )

    vec = vectors[...]
    check_0, check_1, sum_0, sum_1, weight_0, weight_1 = (vec[i : i + 1] for i in range(6))
    rest = sum_0 - mm_nt(weight_1, corner[1])
    pad = jnp.zeros((5, 2 * SIZE), jnp.float32)
    stacked = jnp.concatenate(
        [
            jnp.concatenate([check_0, check_1], axis=1),
            jnp.concatenate([sum_0, sum_1], axis=1),
            jnp.concatenate([rest, sum_1], axis=1),
            pad,
        ]
    )
    solved = mm_nt(stacked, transform)
    new = solved[0:1]
    shift_0 = solved[1:2, :SIZE] + mm_nt(weight_0, upper_0) - weight_0
    shift_1 = solved[2:3, SIZE:] + mm_nt(weight_1, upper_1) - weight_1
    shift = jnp.concatenate([shift_0, shift_1], axis=1)

    row_weights = row_codes[...].astype(jnp.float32) * 0.25
    col_weights = col_codes[...].astype(jnp.float32) * 0.25
    turned = columns_of(row_weights)
    ones = jnp.ones((8, SIZE), jnp.float32)
    fault_row, fault_col = faults[0:1, :], faults[1:2, :]
    magnitude = faults[2:3, :].astype(jnp.float32)

    zero = jnp.zeros((SIZE, SIZE), jnp.float32)
    col_panels, col_hits = [], []
    for u in range(cols):
        raw = jnp.concatenate(
            [gathered(fold * depth + (k * cols + u) * share) for k in range(2)]
        )
        panel = mm(transform, raw)
        if u == 0:
            panel = jnp.concatenate(
                [
                    jnp.where(grid_col > 0, panel[:SIZE], zero),
                    jnp.where(grid_col > 1, panel[SIZE:], zero),
                ]
            )
        col_panels.append(panel)
        col_hits.append(hits(fault_col, (u * grid_cols + grid_col) * SIZE))
        checked = col_sums[u : u + 1, :] - mm(new, panel)
        if u == 0:
            checked = jnp.where(grid_col == 0, new[:, :SIZE], checked)
            checked = jnp.where(grid_col == 1, new[:, SIZE:], checked)
        col_check[u : u + 1, :] = checked

    found = [jnp.zeros((SIZE, SIZE), jnp.float32) for _ in range(cols)]
    found_rows = []
    for t in range(rows):
        h, j = t % fold, t // fold
        raw = jnp.concatenate([gathered(h * depth + (k * cols + j) * share) for k in range(2)])
        panel = mm(transform, raw)
        full = panel
        if t == 0:
            panel = jnp.concatenate(
                [
                    jnp.where(grid_row > 0, panel[:SIZE], zero),
                    jnp.where(grid_row > 1, panel[SIZE:], zero),
                ]
            )
            full = jnp.concatenate(
                [
                    jnp.where(grid_row == 0, upper_0, panel[:SIZE]),
                    jnp.where(grid_row == 1, upper_1, panel[SIZE:]),
                ]
            )
        row_check[t : t + 1, :] = row_sums[t : t + 1, :] - mm(shift, full)
        upright = panel.T
        row_hits = hits(fault_row, (t * grid_rows + grid_row) * SIZE, magnitude)
        total = jnp.zeros((SIZE, SIZE), jnp.float32)
        for u in range(cols):
            where = pl.ds(t * SIZE * cols + u, SIZE, cols)
            tile = matrix[where, :] + fault_tile(row_hits, col_hits[u]) - mm(upright, col_panels[u])
            if u == 0:
                kept = full.T if t == 0 else upright
                tile = jnp.where(grid_col == 0, kept[:, :SIZE], tile)
                tile = jnp.where(grid_col == 1, kept[:, SIZE:], tile)
            if t == 0:
                cleared = (grid_row < 2) & (u * grid_cols + grid_col > grid_row)
                tile = jnp.where(cleared, zero, tile)
            factored[where, :] = tile
            total = total + tile * col_weights[u : u + 1]
            found[u] = found[u] + tile * turned[t]
        found_rows.append(mm_nt(ones, total)[0:1])
    found_rows.append(jnp.zeros((8 - rows, SIZE), jnp.float32))
    found_rows = jnp.concatenate(found_rows)
    found_cols = [jnp.sum(found[u], axis=0, keepdims=True) for u in range(cols)]
    found_cols.append(jnp.zeros((8 - cols, SIZE), jnp.float32))
    found_cols = jnp.concatenate(found_cols)
    for i in range(grid_rows):
        col_message[i] = found_cols
    for i in range(grid_cols):
        row_message[i] = found_rows


def local(matrix, row_codes, col_codes, fault_tiles, fault_cells, fault_bits):
    grid_rows = lax.axis_size("prow")
    grid_cols = lax.axis_size("pcol")
    grid_row = lax.axis_index("prow")
    grid_col = lax.axis_index("pcol")
    rows, _, size, cols, _, _ = matrix.shape
    share = size // grid_rows
    fold = grid_cols // grid_rows
    depth = 2 * cols * share
    geometry = (rows, cols, grid_rows, grid_cols)
    f32 = lambda *shape: jax.ShapeDtypeStruct(shape, jnp.float32)

    flat = matrix.reshape(rows * size * cols, size)
    row_codes = row_codes.reshape(rows, size)
    col_codes = col_codes.reshape(cols, size)
    place = jnp.stack([grid_row, grid_col]).astype(jnp.int32)
    spots = fault_tiles.T * size + fault_cells.T
    magnitude = jnp.left_shift(1, fault_bits - 1)
    faults = jnp.concatenate([spots, magnitude[None]])
    faults = jnp.pad(faults, ((0, 5), (0, size - faults.shape[1])), constant_values=-1)

    message, row_part = pl.pallas_call(
        functools.partial(pre_kernel, geometry),
        out_shape=[f32(grid_rows, cols * share + 8, size), f32(8, size)],
        in_specs=[SMEM] + [VMEM] * 4,
        out_specs=[VMEM] * 2,
        name="pre",
    )(place, faults, flat, row_codes, col_codes)
    first = exchange(message, "prow")
    own_share = first[:2, : cols * share].reshape(depth, size)
    sums = jnp.sum(first[:, cols * share : cols * share + cols], axis=0)
    panel_part = first[:2, cols * share + cols]

    weights = col_codes[:1].astype(jnp.float32) * 0.25
    message = jnp.concatenate([own_share, row_part[:rows], panel_part, sums[:1], weights])
    second = exchange(everyone(message, grid_cols), "pcol")
    shares = second[:, :depth]
    row_sums = jnp.sum(second[:, depth : depth + rows], axis=0)
    panel_sum = jnp.sum(second[:, depth + rows : depth + rows + 2], axis=0)
    ends = second[:2, depth + rows + 2 :]
    vectors = jnp.concatenate([ends[:, 0], panel_sum, ends[:, 1]])

    by_row = shares.reshape(fold, grid_rows, depth, size).transpose(1, 0, 2, 3)
    corner = jnp.concatenate(
        [shares[0, :share], shares[1, :share], shares[1, cols * share : cols * share + share]]
    )
    message = jnp.concatenate(
        [
            by_row.reshape(grid_rows, fold * depth, size),
            everyone(jnp.concatenate([own_share, corner]), grid_rows),
        ],
        axis=1,
    )
    third = exchange(message, "prow")

    factored, col_check, row_check, col_message, row_message = pl.pallas_call(
        functools.partial(post_kernel, geometry),
        out_shape=[
            f32(rows * size * cols, size),
            f32(cols, size),
            f32(rows, size),
            f32(grid_rows, 8, size),
            f32(grid_cols, 8, size),
        ],
        in_specs=[SMEM] + [VMEM] * 8,
        out_specs=[VMEM] * 5,
        name="post",
    )(place, faults, third, vectors, row_sums, sums, flat, row_codes, col_codes)

    col_found = jnp.sum(exchange(col_message, "prow"), axis=0)[:cols]
    row_found = jnp.sum(exchange(row_message, "pcol"), axis=0)[:rows]
    col_flags = jnp.max(jnp.abs(col_check - col_found), axis=1)
    row_flags = jnp.max(jnp.abs(row_check - row_found), axis=1)
    return (
        factored.reshape(matrix.shape),
        col_check.reshape(cols, 1, size),
        row_check.reshape(rows, 1, size),
        col_flags.reshape(cols, 1),
        row_flags.reshape(rows, 1),
    )


def solution(mesh):
    return jax.shard_map(
        local,
        mesh=mesh,
        in_specs=(
            P(None, "prow", None, None, "pcol", None),
            P(None, "prow", None),
            P(None, "pcol", None),
            P(),
            P(),
            P(),
        ),
        out_specs=(
            P(None, "prow", None, None, "pcol", None),
            P(None, "pcol", None),
            P(None, "prow", None),
            P(None, "pcol"),
            P(None, "prow"),
        ),
        check_vma=False,
    )
```

```python
import functools

import jax
import jax.numpy as jnp
from jax import lax
from jax.experimental import pallas as pl
from jax.experimental.pallas import tpu as pltpu
from jax.sharding import PartitionSpec as P

SIZE = 128
GROUP = 8
precise = lax.Precision.HIGHEST
VMEM = pl.BlockSpec(memory_space=pltpu.VMEM)
SMEM = pl.BlockSpec(memory_space=pltpu.SMEM)


def exchange(message, axis):
    return lax.all_to_all(message, axis, 0, 0, tiled=True)


def everyone(part, count):
    return jnp.broadcast_to(part[None], (count,) + part.shape)


def mm(a, b):
    return jnp.dot(a, b, precision=precise, preferred_element_type=jnp.float32)


def mm_nt(a, b):
    return lax.dot_general(
        a, b, (((1,), (1,)), ((), ())), precision=precise, preferred_element_type=jnp.float32
    )


def factor_tile(tile):
    lanes = lambda v, c: jnp.broadcast_to(v[:, c : c + 1], v.shape)
    rows = lambda v, j: jnp.broadcast_to(v[j : j + 1, :], v.shape)
    groups = SIZE // GROUP
    sub = lax.broadcasted_iota(jnp.int32, (GROUP, SIZE), 0)
    lan = lax.broadcasted_iota(jnp.int32, (GROUP, SIZE), 1)
    left = [tile[GROUP * i : GROUP * (i + 1), :] for i in range(groups)]
    right = [jnp.where(lan == sub + GROUP * i, 1.0, 0.0) for i in range(groups)]
    upper, inverse = [], []
    for b in range(groups):
        first = GROUP * b
        column = [lanes(left[b], first + j) for j in range(GROUP)]
        d = [[rows(column[j], i) if j <= i else None for j in range(GROUP)] for i in range(GROUP)]
        ra = [rows(left[b], j) for j in range(GROUP)]
        rb = [rows(right[b], j) for j in range(GROUP)]
        scale = []
        for k in range(GROUP):
            scale.append(lax.rsqrt(d[k][k]))
            for i in range(k + 1, GROUP):
                d[i][k] = d[i][k] * scale[k]
            for j in range(k + 1, GROUP):
                for i in range(j, GROUP):
                    d[i][j] = d[i][j] - d[i][k] * d[j][k]
        for j in range(GROUP):
            for k in range(j):
                ra[j] = ra[j] - d[j][k] * ra[k]
                rb[j] = rb[j] - d[j][k] * rb[k]
            ra[j] = ra[j] * scale[j]
            rb[j] = rb[j] * scale[j]
        for i in range(b + 1, groups):
            c = [lanes(left[i], first + j) for j in range(GROUP)]
            for j in range(GROUP):
                for k in range(j):
                    c[j] = c[j] - d[j][k] * c[k]
                c[j] = c[j] * scale[j]
            for j in range(GROUP):
                left[i] = left[i] - c[j] * ra[j]
                right[i] = right[i] - c[j] * rb[j]
        out_a, out_b = ra[GROUP - 1], rb[GROUP - 1]
        for j in range(GROUP - 1):
            out_a = jnp.where(sub == j, ra[j], out_a)
            out_b = jnp.where(sub == j, rb[j], out_b)
        upper.append(jnp.where(lan >= sub + first, out_a, 0.0))
        inverse.append(out_b)
    return jnp.concatenate(upper), jnp.concatenate(inverse)


def columns_of(weights):
    count = weights.shape[0]
    padded = jnp.concatenate([weights, jnp.zeros((SIZE - count, SIZE), jnp.float32)])
    turned = padded.T
    return [jnp.broadcast_to(turned[:, t : t + 1], (SIZE, SIZE)) for t in range(count)]


def hits(fault_row, first, scale=None):
    place = first + lax.broadcasted_iota(jnp.int32, (SIZE, SIZE), 0)
    found = jnp.where(fault_row == place, 1.0 if scale is None else scale, 0.0)
    return found.astype(jnp.bfloat16)


def fault_tile(row_hits, col_hits):
    return lax.dot_general(
        row_hits, col_hits, (((1,), (1,)), ((), ())), preferred_element_type=jnp.float32
    )


def stacked_rows(ref):
    return jnp.concatenate([ref[i] for i in range(ref.shape[0])])


def pre_kernel(
    geometry,
    place,
    fault_tiles,
    fault_cells,
    fault_bits,
    matrix,
    row_codes,
    col_codes,
    message,
    row_part,
    faults,
):
    rows, cols, grid_rows, grid_cols = geometry
    grid_row, grid_col = place[0], place[1]
    share = SIZE // grid_rows
    count = fault_bits.shape[1]
    faults[...] = jnp.full((8, SIZE), -1, jnp.int32)
    faults[0:2, 0:count] = fault_tiles[...] * SIZE + fault_cells[...]
    faults[2:3, 0:count] = jnp.left_shift(jnp.ones((1, count), jnp.int32), fault_bits[...] - 1)
    row_weights = stacked_rows(row_codes).astype(jnp.float32) * 0.25
    col_weights = stacked_rows(col_codes).astype(jnp.float32) * 0.25
    turned = columns_of(row_weights)
    ones = jnp.ones((8, SIZE), jnp.float32)
    fault_row, fault_col = faults[0:1, :], faults[1:2, :]
    magnitude = faults[2:3, :].astype(jnp.float32)
    mirror_rows = hits(fault_col, grid_row * SIZE)
    col_sums = [jnp.zeros((SIZE, SIZE), jnp.float32) for _ in range(cols)]
    panel = jnp.zeros((SIZE, SIZE), jnp.float32)
    for t in range(rows):
        total = jnp.zeros((SIZE, SIZE), jnp.float32)
        for u in range(cols):
            tile = matrix[pl.ds(t * SIZE * cols + u, SIZE, cols), :]
            weight = col_weights[u : u + 1]
            total = total + tile * weight
            col_sums[u] = col_sums[u] + tile * turned[t]
            if t == 0:
                col_tile = u * grid_cols + grid_col
                tile = tile + fault_tile(mirror_rows, hits(fault_row, col_tile * SIZE, magnitude))
                panel = panel + tile * jnp.where(col_tile > grid_row, weight, 0.0)
                for i in range(grid_rows):
                    message[i, u * share : (u + 1) * share, :] = tile[i * share : (i + 1) * share]
        row_part[t : t + 1, :] = mm_nt(ones, total)[0:1]
    row_part[rows:8, :] = jnp.zeros((8 - rows, SIZE), jnp.float32)
    sums = [jnp.sum(col_sums[u], axis=0, keepdims=True) for u in range(cols)]
    sums.append(mm_nt(ones, panel)[0:1])
    sums.append(jnp.zeros((8 - cols - 1, SIZE), jnp.float32))
    sums = jnp.concatenate(sums)
    for i in range(grid_rows):
        message[i, cols * share : cols * share + 8, :] = sums


def factor_kernel(geometry, corners, vectors, transform, uppers, pair):
    grid_rows = geometry[2]
    share = SIZE // grid_rows
    def gathered(start):
        return jnp.concatenate([corners[i, start : start + share, :] for i in range(grid_rows)])

    corner = [gathered(k * share) for k in range(3)]
    tile_0 = (corner[0] + corner[0].T) * 0.5
    upper_0, inverse_0 = factor_tile(tile_0)
    below_0 = mm(inverse_0, corner[1])
    tile_1 = corner[2] - mm(below_0.T, below_0)
    upper_1, inverse_1 = factor_tile((tile_1 + tile_1.T) * 0.5)
    mixed = -mm(inverse_1, mm(below_0.T, inverse_0))
    whole = jnp.concatenate(
        [
            jnp.concatenate([inverse_0, jnp.zeros_like(inverse_0)], axis=1),
            jnp.concatenate([mixed, inverse_1], axis=1),
        ]
    )

    vec = vectors[...]
    check_0, check_1, sum_0, sum_1, weight_0, weight_1 = (vec[i : i + 1] for i in range(6))
    rest = sum_0 - mm_nt(weight_1, corner[1])
    pad = jnp.zeros((5, 2 * SIZE), jnp.float32)
    stacked = jnp.concatenate(
        [
            jnp.concatenate([check_0, check_1], axis=1),
            jnp.concatenate([sum_0, sum_1], axis=1),
            jnp.concatenate([rest, sum_1], axis=1),
            pad,
        ]
    )
    solved = mm_nt(stacked, whole)
    shift_0 = solved[1:2, :SIZE] + mm_nt(weight_0, upper_0) - weight_0
    shift_1 = solved[2:3, SIZE:] + mm_nt(weight_1, upper_1) - weight_1
    shift = jnp.concatenate([shift_0, shift_1], axis=1)
    transform[...] = whole
    uppers[0] = upper_0
    uppers[1] = upper_1
    pair[...] = jnp.concatenate([solved[0:1], shift, jnp.zeros((6, 2 * SIZE), jnp.float32)])


def post_kernel(
    geometry,
    place,
    faults,
    third,
    transform,
    uppers,
    pair,
    row_part,
    col_sums,
    matrix,
    row_codes,
    col_codes,
    factored,
    col_check,
    row_shift,
    col_message,
    row_message,
):
    rows, cols, grid_rows, grid_cols = geometry
    grid_row, grid_col = place[0], place[1]
    share = SIZE // grid_rows
    fold = grid_cols // grid_rows
    depth = 2 * cols * share

    def gathered(start):
        return jnp.concatenate([third[i, start : start + share, :] for i in range(grid_rows)])

    transform = transform[...]
    upper_0, upper_1 = uppers[0], uppers[1]
    new, shift = pair[0:1, :], pair[1:2, :]
    row_weights = stacked_rows(row_codes).astype(jnp.float32) * 0.25
    col_weights = stacked_rows(col_codes).astype(jnp.float32) * 0.25
    turned = columns_of(row_weights)
    ones = jnp.ones((8, SIZE), jnp.float32)
    fault_row, fault_col = faults[0:1, :], faults[1:2, :]
    magnitude = faults[2:3, :].astype(jnp.float32)

    zero = jnp.zeros((SIZE, SIZE), jnp.float32)
    col_panels, col_hits = [], []
    for u in range(cols):
        raw = jnp.concatenate(
            [gathered(fold * depth + (k * cols + u) * share) for k in range(2)]
        )
        panel = mm(transform, raw)
        if u == 0:
            panel = jnp.concatenate(
                [
                    jnp.where(grid_col > 0, panel[:SIZE], zero),
                    jnp.where(grid_col > 1, panel[SIZE:], zero),
                ]
            )
        col_panels.append(panel)
        col_hits.append(hits(fault_col, (u * grid_cols + grid_col) * SIZE))
        checked = col_sums[u : u + 1, :] - mm(new, panel)
        if u == 0:
            checked = jnp.where(grid_col == 0, new[:, :SIZE], checked)
            checked = jnp.where(grid_col == 1, new[:, SIZE:], checked)
        col_check[u] = checked

    found = [jnp.zeros((SIZE, SIZE), jnp.float32) for _ in range(cols)]
    found_rows = []
    for t in range(rows):
        h, j = t % fold, t // fold
        raw = jnp.concatenate([gathered(h * depth + (k * cols + j) * share) for k in range(2)])
        panel = mm(transform, raw)
        full = panel
        if t == 0:
            panel = jnp.concatenate(
                [
                    jnp.where(grid_row > 0, panel[:SIZE], zero),
                    jnp.where(grid_row > 1, panel[SIZE:], zero),
                ]
            )
            full = jnp.concatenate(
                [
                    jnp.where(grid_row == 0, upper_0, panel[:SIZE]),
                    jnp.where(grid_row == 1, upper_1, panel[SIZE:]),
                ]
            )
        row_shift[t] = mm(shift, full)
        upright = panel.T
        row_hits = hits(fault_row, (t * grid_rows + grid_row) * SIZE, magnitude)
        total = jnp.zeros((SIZE, SIZE), jnp.float32)
        for u in range(cols):
            where = pl.ds(t * SIZE * cols + u, SIZE, cols)
            tile = matrix[where, :] + fault_tile(row_hits, col_hits[u]) - mm(upright, col_panels[u])
            if u == 0:
                kept = full.T if t == 0 else upright
                tile = jnp.where(grid_col == 0, kept[:, :SIZE], tile)
                tile = jnp.where(grid_col == 1, kept[:, SIZE:], tile)
            if t == 0:
                cleared = (grid_row < 2) & (u * grid_cols + grid_col > grid_row)
                tile = jnp.where(cleared, zero, tile)
            factored[where, :] = tile
            total = total + tile * col_weights[u : u + 1]
            found[u] = found[u] + tile * turned[t]
        found_rows.append(mm_nt(ones, total)[0:1])
    found_rows.append(jnp.zeros((8 - rows, SIZE), jnp.float32))
    found_rows = jnp.concatenate(found_rows)
    found_cols = [jnp.sum(found[u], axis=0, keepdims=True) for u in range(cols)]
    found_cols.append(jnp.zeros((8 - cols, SIZE), jnp.float32))
    found_cols = jnp.concatenate(found_cols)
    for i in range(grid_rows):
        col_message[i] = found_cols
    for i in range(grid_cols):
        row_message[i, 0:8, :] = found_rows
        row_message[i, 8:16, :] = row_part[...]


def local(matrix, row_codes, col_codes, fault_tiles, fault_cells, fault_bits):
    grid_rows = lax.axis_size("prow")
    grid_cols = lax.axis_size("pcol")
    grid_row = lax.axis_index("prow")
    grid_col = lax.axis_index("pcol")
    rows, _, size, cols, _, _ = matrix.shape
    share = size // grid_rows
    fold = grid_cols // grid_rows
    depth = 2 * cols * share
    geometry = (rows, cols, grid_rows, grid_cols)
    f32 = lambda *shape: jax.ShapeDtypeStruct(shape, jnp.float32)

    flat = matrix.reshape(rows * size * cols, size)
    place = jnp.stack([grid_row, grid_col]).astype(jnp.int32)

    message, row_part, faults = pl.pallas_call(
        functools.partial(pre_kernel, geometry),
        out_shape=[
            f32(grid_rows, cols * share + 8, size),
            f32(8, size),
            jax.ShapeDtypeStruct((8, size), jnp.int32),
        ],
        in_specs=[SMEM] + [VMEM] * 6,
        out_specs=[VMEM] * 3,
        name="pre",
    )(place, fault_tiles.T, fault_cells.T, fault_bits[None], flat, row_codes, col_codes)
    first = exchange(message, "prow")
    own_share = first[:2, : cols * share].reshape(depth, size)
    sums = jnp.sum(first[:, cols * share : cols * share + cols], axis=0)
    panel_part = first[:2, cols * share + cols]

    weights = col_codes[0].astype(jnp.float32) * 0.25
    message = jnp.concatenate([own_share, panel_part, sums[:1], weights])
    second = exchange(everyone(message, grid_cols), "pcol")
    shares = second[:, :depth]
    panel_sum = jnp.sum(second[:, depth : depth + 2], axis=0)
    ends = second[:2, depth + 2 :]
    vectors = jnp.concatenate([ends[:, 0], panel_sum, ends[:, 1]])

    corner = jnp.concatenate(
        [shares[0, :share], shares[1, :share], shares[1, cols * share : cols * share + share]]
    )
    corners = exchange(everyone(corner, grid_rows), "prow")
    by_row = shares.reshape(fold, grid_rows, depth, size).transpose(1, 0, 2, 3)
    message = jnp.concatenate(
        [by_row.reshape(grid_rows, fold * depth, size), everyone(own_share, grid_rows)], axis=1
    )
    message, corners = lax.optimization_barrier((message, corners))
    third = exchange(message, "prow")
    transform, uppers, pair = pl.pallas_call(
        functools.partial(factor_kernel, geometry),
        out_shape=[f32(2 * size, 2 * size), f32(2, size, size), f32(8, 2 * size)],
        in_specs=[VMEM] * 2,
        out_specs=[VMEM] * 3,
        name="factor",
    )(corners, vectors)

    factored, col_check, row_shift, col_message, row_message = pl.pallas_call(
        functools.partial(post_kernel, geometry),
        out_shape=[
            f32(rows * size * cols, size),
            f32(cols, 1, size),
            f32(rows, 1, size),
            f32(grid_rows, 8, size),
            f32(grid_cols, 16, size),
        ],
        in_specs=[SMEM] + [VMEM] * 10,
        out_specs=[VMEM] * 5,
        name="post",
    )(place, faults, third, transform, uppers, pair, row_part, sums, flat, row_codes, col_codes)

    row_found = exchange(row_message, "pcol")
    col_message, row_found = lax.optimization_barrier((col_message, row_found))
    col_found = exchange(col_message, "prow")
    row_found = jnp.sum(row_found, axis=0)
    row_check = row_found[8 : 8 + rows] - row_shift.reshape(rows, size)
    row_flags = jnp.max(jnp.abs(row_check - row_found[:rows]), axis=1)
    col_found = jnp.sum(col_found, axis=0)[:cols]
    col_flags = jnp.max(jnp.abs(col_check.reshape(cols, size) - col_found), axis=1)
    return (
        factored.reshape(matrix.shape),
        col_check,
        row_check.reshape(rows, 1, size),
        col_flags.reshape(cols, 1),
        row_flags.reshape(rows, 1),
    )


def solution(mesh):
    return jax.shard_map(
        local,
        mesh=mesh,
        in_specs=(
            P(None, "prow", None, None, "pcol", None),
            P(None, "prow", None),
            P(None, "pcol", None),
            P(),
            P(),
            P(),
        ),
        out_specs=(
            P(None, "prow", None, None, "pcol", None),
            P(None, "pcol", None),
            P(None, "prow", None),
            P(None, "pcol"),
            P(None, "prow"),
        ),
        check_vma=False,
    )
```

```python
import functools

import jax
import jax.numpy as jnp
from jax import lax
from jax.experimental import pallas as pl
from jax.experimental.pallas import tpu as pltpu
from jax.sharding import PartitionSpec as P

SIZE = 128
GROUP = 8
precise = lax.Precision.HIGHEST
VMEM = pl.BlockSpec(memory_space=pltpu.VMEM)
SMEM = pl.BlockSpec(memory_space=pltpu.SMEM)


def exchange(message, axis):
    return lax.all_to_all(message, axis, 0, 0, tiled=True)


def everyone(part, count):
    return jnp.broadcast_to(part[None], (count,) + part.shape)


def mm(a, b):
    return jnp.dot(a, b, precision=precise, preferred_element_type=jnp.float32)


def mm_nt(a, b):
    return lax.dot_general(
        a, b, (((1,), (1,)), ((), ())), precision=precise, preferred_element_type=jnp.float32
    )


def factor_tile(tile):
    lanes = lambda v, c: jnp.broadcast_to(v[:, c : c + 1], v.shape)
    rows = lambda v, j: jnp.broadcast_to(v[j : j + 1, :], v.shape)
    groups = SIZE // GROUP
    sub = lax.broadcasted_iota(jnp.int32, (GROUP, SIZE), 0)
    lan = lax.broadcasted_iota(jnp.int32, (GROUP, SIZE), 1)
    left = [tile[GROUP * i : GROUP * (i + 1), :] for i in range(groups)]
    right = [jnp.where(lan == sub + GROUP * i, 1.0, 0.0) for i in range(groups)]
    upper, inverse = [], []
    for b in range(groups):
        first = GROUP * b
        column = [lanes(left[b], first + j) for j in range(GROUP)]
        d = [[rows(column[j], i) if j <= i else None for j in range(GROUP)] for i in range(GROUP)]
        ra = [rows(left[b], j) for j in range(GROUP)]
        rb = [rows(right[b], j) for j in range(GROUP)]
        scale = []
        for k in range(GROUP):
            scale.append(lax.rsqrt(d[k][k]))
            for i in range(k + 1, GROUP):
                d[i][k] = d[i][k] * scale[k]
            for j in range(k + 1, GROUP):
                for i in range(j, GROUP):
                    d[i][j] = d[i][j] - d[i][k] * d[j][k]
        for j in range(GROUP):
            for k in range(j):
                ra[j] = ra[j] - d[j][k] * ra[k]
                rb[j] = rb[j] - d[j][k] * rb[k]
            ra[j] = ra[j] * scale[j]
            rb[j] = rb[j] * scale[j]
        for i in range(b + 1, groups):
            c = [lanes(left[i], first + j) for j in range(GROUP)]
            for j in range(GROUP):
                for k in range(j):
                    c[j] = c[j] - d[j][k] * c[k]
                c[j] = c[j] * scale[j]
            for j in range(GROUP):
                left[i] = left[i] - c[j] * ra[j]
                right[i] = right[i] - c[j] * rb[j]
        out_a, out_b = ra[GROUP - 1], rb[GROUP - 1]
        for j in range(GROUP - 1):
            out_a = jnp.where(sub == j, ra[j], out_a)
            out_b = jnp.where(sub == j, rb[j], out_b)
        upper.append(jnp.where(lan >= sub + first, out_a, 0.0))
        inverse.append(out_b)
    return jnp.concatenate(upper), jnp.concatenate(inverse)


def columns_of(weights):
    count = weights.shape[0]
    padded = jnp.concatenate([weights, jnp.zeros((SIZE - count, SIZE), jnp.float32)])
    turned = padded.T
    return [jnp.broadcast_to(turned[:, t : t + 1], (SIZE, SIZE)) for t in range(count)]


def hits(fault_row, first, scale=None):
    place = first + lax.broadcasted_iota(jnp.int32, (SIZE, SIZE), 0)
    found = jnp.where(fault_row == place, 1.0 if scale is None else scale, 0.0)
    return found.astype(jnp.bfloat16)


def fault_tile(row_hits, col_hits):
    return lax.dot_general(
        row_hits, col_hits, (((1,), (1,)), ((), ())), preferred_element_type=jnp.float32
    )


def stacked_rows(ref):
    return jnp.concatenate([ref[i] for i in range(ref.shape[0])])


def pre_kernel(
    geometry,
    place,
    fault_tiles,
    fault_cells,
    fault_bits,
    matrix,
    row_codes,
    col_codes,
    message,
    row_part,
    faults,
):
    rows, cols, grid_rows, grid_cols = geometry
    grid_row, grid_col = place[0], place[1]
    share = SIZE // grid_rows
    count = fault_bits.shape[1]
    faults[...] = jnp.full((8, SIZE), -1, jnp.int32)
    faults[0:2, 0:count] = fault_tiles[...] * SIZE + fault_cells[...]
    faults[2:3, 0:count] = jnp.left_shift(jnp.ones((1, count), jnp.int32), fault_bits[...] - 1)
    row_weights = stacked_rows(row_codes).astype(jnp.float32) * 0.25
    col_weights = stacked_rows(col_codes).astype(jnp.float32) * 0.25
    turned = columns_of(row_weights)
    ones = jnp.ones((8, SIZE), jnp.float32)
    fault_row, fault_col = faults[0:1, :], faults[1:2, :]
    magnitude = faults[2:3, :].astype(jnp.float32)
    mirror_rows = hits(fault_col, grid_row * SIZE)
    col_sums = [jnp.zeros((SIZE, SIZE), jnp.float32) for _ in range(cols)]
    panel = jnp.zeros((SIZE, SIZE), jnp.float32)
    for t in range(rows):
        total = jnp.zeros((SIZE, SIZE), jnp.float32)
        for u in range(cols):
            tile = matrix[pl.ds(t * SIZE * cols + u, SIZE, cols), :]
            weight = col_weights[u : u + 1]
            total = total + tile * weight
            col_sums[u] = col_sums[u] + tile * turned[t]
            if t == 0:
                col_tile = u * grid_cols + grid_col
                tile = tile + fault_tile(mirror_rows, hits(fault_row, col_tile * SIZE, magnitude))
                panel = panel + tile * jnp.where(col_tile > grid_row, weight, 0.0)
                for i in range(grid_rows):
                    message[i, u * share : (u + 1) * share, :] = tile[i * share : (i + 1) * share]
        row_part[t : t + 1, :] = mm_nt(ones, total)[0:1]
    row_part[rows:8, :] = jnp.zeros((8 - rows, SIZE), jnp.float32)
    sums = [jnp.sum(col_sums[u], axis=0, keepdims=True) for u in range(cols)]
    sums.append(mm_nt(ones, panel)[0:1])
    sums.append(jnp.zeros((8 - cols - 1, SIZE), jnp.float32))
    sums = jnp.concatenate(sums)
    for i in range(grid_rows):
        message[i, cols * share : cols * share + 8, :] = sums


def factor_kernel(geometry, corners, vectors, transform, uppers, pair):
    grid_rows = geometry[2]
    share = SIZE // grid_rows
    def gathered(start):
        return jnp.concatenate([corners[i, start : start + share, :] for i in range(grid_rows)])

    corner = [gathered(k * share) for k in range(3)]
    tile_0 = (corner[0] + corner[0].T) * 0.5
    upper_0, inverse_0 = factor_tile(tile_0)
    below_0 = mm(inverse_0, corner[1])
    tile_1 = corner[2] - mm(below_0.T, below_0)
    upper_1, inverse_1 = factor_tile((tile_1 + tile_1.T) * 0.5)
    mixed = -mm(inverse_1, mm(below_0.T, inverse_0))
    whole = jnp.concatenate(
        [
            jnp.concatenate([inverse_0, jnp.zeros_like(inverse_0)], axis=1),
            jnp.concatenate([mixed, inverse_1], axis=1),
        ]
    )

    vec = vectors[...]
    check_0, check_1, sum_0, sum_1, weight_0, weight_1 = (vec[i : i + 1] for i in range(6))
    rest = sum_0 - mm_nt(weight_1, corner[1])
    pad = jnp.zeros((5, 2 * SIZE), jnp.float32)
    stacked = jnp.concatenate(
        [
            jnp.concatenate([check_0, check_1], axis=1),
            jnp.concatenate([sum_0, sum_1], axis=1),
            jnp.concatenate([rest, sum_1], axis=1),
            pad,
        ]
    )
    solved = mm_nt(stacked, whole)
    shift_0 = solved[1:2, :SIZE] + mm_nt(weight_0, upper_0) - weight_0
    shift_1 = solved[2:3, SIZE:] + mm_nt(weight_1, upper_1) - weight_1
    shift = jnp.concatenate([shift_0, shift_1], axis=1)
    transform[...] = whole
    uppers[0] = upper_0
    uppers[1] = upper_1
    pair[...] = jnp.concatenate([solved[0:1], shift, jnp.zeros((6, 2 * SIZE), jnp.float32)])


def post_kernel(
    geometry,
    early,
    place,
    faults,
    third,
    transform,
    uppers,
    pair,
    row_part,
    col_sums,
    matrix,
    row_codes,
    col_codes,
    factored,
    col_check,
    row_shift,
    col_message,
    row_message,
):
    rows, cols, grid_rows, grid_cols = geometry
    grid_row, grid_col = place[0], place[1]
    share = SIZE // grid_rows
    fold = grid_cols // grid_rows
    depth = 2 * cols * share

    def gathered(start):
        return jnp.concatenate([third[i, start : start + share, :] for i in range(grid_rows)])

    transform = transform[...]
    upper_0, upper_1 = uppers[0], uppers[1]
    new, shift = pair[0:1, :], pair[1:2, :]
    row_weights = stacked_rows(row_codes).astype(jnp.float32) * 0.25
    col_weights = stacked_rows(col_codes).astype(jnp.float32) * 0.25
    turned = columns_of(row_weights)
    ones = jnp.ones((8, SIZE), jnp.float32)
    fault_row, fault_col = faults[0:1, :], faults[1:2, :]
    magnitude = faults[2:3, :].astype(jnp.float32)

    zero = jnp.zeros((SIZE, SIZE), jnp.float32)
    col_panels, col_hits = [], []
    for u in range(cols):
        raw = jnp.concatenate(
            [gathered(fold * depth + (k * cols + u) * share) for k in range(2)]
        )
        panel = mm(transform, raw)
        if u == 0:
            panel = jnp.concatenate(
                [
                    jnp.where(grid_col > 0, panel[:SIZE], zero),
                    jnp.where(grid_col > 1, panel[SIZE:], zero),
                ]
            )
        col_panels.append(panel)
        col_hits.append(hits(fault_col, (u * grid_cols + grid_col) * SIZE))
        checked = col_sums[u : u + 1, :] - mm(new, panel)
        if u == 0:
            checked = jnp.where(grid_col == 0, new[:, :SIZE], checked)
            checked = jnp.where(grid_col == 1, new[:, SIZE:], checked)
        col_check[u] = checked

    found = [jnp.zeros((SIZE, SIZE), jnp.float32) for _ in range(cols)]
    found_rows = []
    for t in range(rows):
        h, j = t % fold, t // fold
        raw = jnp.concatenate([gathered(h * depth + (k * cols + j) * share) for k in range(2)])
        panel = mm(transform, raw)
        full = panel
        if t == 0:
            panel = jnp.concatenate(
                [
                    jnp.where(grid_row > 0, panel[:SIZE], zero),
                    jnp.where(grid_row > 1, panel[SIZE:], zero),
                ]
            )
            full = jnp.concatenate(
                [
                    jnp.where(grid_row == 0, upper_0, panel[:SIZE]),
                    jnp.where(grid_row == 1, upper_1, panel[SIZE:]),
                ]
            )
        row_shift[t] = mm(shift, full)
        upright = panel.T
        row_hits = hits(fault_row, (t * grid_rows + grid_row) * SIZE, magnitude)
        total = jnp.zeros((SIZE, SIZE), jnp.float32)
        for u in range(cols):
            where = pl.ds(t * SIZE * cols + u, SIZE, cols)
            tile = matrix[where, :] + fault_tile(row_hits, col_hits[u]) - mm(upright, col_panels[u])
            if u == 0:
                kept = full.T if t == 0 else upright
                tile = jnp.where(grid_col == 0, kept[:, :SIZE], tile)
                tile = jnp.where(grid_col == 1, kept[:, SIZE:], tile)
            if t == 0:
                cleared = (grid_row < 2) & (u * grid_cols + grid_col > grid_row)
                tile = jnp.where(cleared, zero, tile)
            factored[where, :] = tile
            total = total + tile * col_weights[u : u + 1]
            found[u] = found[u] + tile * turned[t]
        found_rows.append(mm_nt(ones, total)[0:1])
    found_rows.append(row_part[early:rows, :])
    if (2 * rows - early) % 8:
        found_rows.append(jnp.zeros(((early - 2 * rows) % 8, SIZE), jnp.float32))
    found_rows = jnp.concatenate(found_rows)
    found_cols = [jnp.sum(found[u], axis=0, keepdims=True) for u in range(cols)]
    found_cols.append(jnp.zeros((8 - cols, SIZE), jnp.float32))
    found_cols = jnp.concatenate(found_cols)
    for i in range(grid_rows):
        col_message[i] = found_cols
    for i in range(grid_cols):
        row_message[i] = found_rows


def local(matrix, row_codes, col_codes, fault_tiles, fault_cells, fault_bits):
    grid_rows = lax.axis_size("prow")
    grid_cols = lax.axis_size("pcol")
    grid_row = lax.axis_index("prow")
    grid_col = lax.axis_index("pcol")
    rows, _, size, cols, _, _ = matrix.shape
    share = size // grid_rows
    fold = grid_cols // grid_rows
    depth = 2 * cols * share
    geometry = (rows, cols, grid_rows, grid_cols)
    f32 = lambda *shape: jax.ShapeDtypeStruct(shape, jnp.float32)

    flat = matrix.reshape(rows * size * cols, size)
    place = jnp.stack([grid_row, grid_col]).astype(jnp.int32)

    message, row_part, faults = pl.pallas_call(
        functools.partial(pre_kernel, geometry),
        out_shape=[
            f32(grid_rows, cols * share + 8, size),
            f32(8, size),
            jax.ShapeDtypeStruct((8, size), jnp.int32),
        ],
        in_specs=[SMEM] + [VMEM] * 6,
        out_specs=[VMEM] * 3,
        name="pre",
    )(place, fault_tiles.T, fault_cells.T, fault_bits[None], flat, row_codes, col_codes)
    first = exchange(message, "prow")
    own_share = first[:2, : cols * share].reshape(depth, size)
    sums = jnp.sum(first[:, cols * share : cols * share + cols], axis=0)
    panel_part = first[:2, cols * share + cols]

    weights = col_codes[0].astype(jnp.float32) * 0.25
    early = min(rows - 1, -(depth + 4) % 8)
    message = jnp.concatenate([own_share, panel_part, sums[:1], weights, row_part[:early]])
    second = exchange(everyone(message, grid_cols), "pcol")
    shares = second[:, :depth]
    panel_sum = jnp.sum(second[:, depth : depth + 2], axis=0)
    ends = second[:2, depth + 2 : depth + 4]
    early_sums = jnp.sum(second[:, depth + 4 :], axis=0)
    vectors = jnp.concatenate([ends[:, 0], panel_sum, ends[:, 1]])

    corner = jnp.concatenate(
        [shares[0, :share], shares[1, :share], shares[1, cols * share : cols * share + share]]
    )
    corners = exchange(everyone(corner, grid_rows), "prow")
    by_row = shares.reshape(fold, grid_rows, depth, size).transpose(1, 0, 2, 3)
    message = jnp.concatenate(
        [by_row.reshape(grid_rows, fold * depth, size), everyone(own_share, grid_rows)], axis=1
    )
    message, corners = lax.optimization_barrier((message, corners))
    third = exchange(message, "prow")
    transform, uppers, pair = pl.pallas_call(
        functools.partial(factor_kernel, geometry),
        out_shape=[f32(2 * size, 2 * size), f32(2, size, size), f32(8, 2 * size)],
        in_specs=[VMEM] * 2,
        out_specs=[VMEM] * 3,
        name="factor",
    )(corners, vectors)

    factored, col_check, row_shift, col_message, row_message = pl.pallas_call(
        functools.partial(post_kernel, geometry, early),
        out_shape=[
            f32(rows * size * cols, size),
            f32(cols, 1, size),
            f32(rows, 1, size),
            f32(grid_rows, 8, size),
            f32(grid_cols, 2 * rows - early + (early - 2 * rows) % 8, size),
        ],
        in_specs=[SMEM] + [VMEM] * 10,
        out_specs=[VMEM] * 5,
        name="post",
    )(place, faults, third, transform, uppers, pair, row_part, sums, flat, row_codes, col_codes)

    row_found = exchange(row_message, "pcol")
    col_message, row_found = lax.optimization_barrier((col_message, row_found))
    col_found = exchange(col_message, "prow")
    row_found = jnp.sum(row_found, axis=0)
    row_sums = jnp.concatenate([early_sums, row_found[rows : 2 * rows - early]])
    row_check = row_sums - row_shift.reshape(rows, size)
    row_flags = jnp.max(jnp.abs(row_check - row_found[:rows]), axis=1)
    col_found = jnp.sum(col_found, axis=0)[:cols]
    col_flags = jnp.max(jnp.abs(col_check.reshape(cols, size) - col_found), axis=1)
    return (
        factored.reshape(matrix.shape),
        col_check,
        row_check.reshape(rows, 1, size),
        col_flags.reshape(cols, 1),
        row_flags.reshape(rows, 1),
    )


def solution(mesh):
    return jax.shard_map(
        local,
        mesh=mesh,
        in_specs=(
            P(None, "prow", None, None, "pcol", None),
            P(None, "prow", None),
            P(None, "pcol", None),
            P(),
            P(),
            P(),
        ),
        out_specs=(
            P(None, "prow", None, None, "pcol", None),
            P(None, "pcol", None),
            P(None, "prow", None),
            P(None, "pcol"),
            P(None, "prow"),
        ),
        check_vma=False,
    )
```
